256 devices in a mesh: nodes: 128 (over y, z, x), params: 2 (over core).
Axes of the slice: x: 4, y: 4, z: 8, core: 2. Of those that a mesh axis runs over, the one named last changes fastest.
Arguments:
- snapshots: bfloat16 [128, 48, 131072], P('params', None, 'nodes'), may hold values from -6 to 6
- space_start: float32 [64, 131072], P(None, 'nodes'), may hold values from -12 to 12
- time_start: float32 [64, 48], replicated, may hold values from -0.9 to 0.9
Outputs:
- space_factor: float32 [64, 131072], P(None, 'nodes')
- param_factor: float32 [64, 128], P(None, 'params')
- time_factor: float32 [64, 48], replicated
The draws below stay inside these ranges and needn't reach their ends.
All inputs are finite; a program needn't handle non-finite values.
Results may differ from the reference program's by a relative error of at most 0.0093.
Values sent between devices are 32-bit elements; how exact they have to be, the bound alone decides.
No kernel may reach another device: no remote copies, remote signals or barrier semaphores. Data moves between devices by JAX's collectives and lax.ppermute only.
A program may use at most 64 MiB of HBM per device.

```python
import math
import jax
import jax.numpy as jnp
from jax import lax

PARAMS = 128
TIMES = 48
RANK = 64
SWEEPS = 4
NODES = 131072


def draw_space_start(key, part):
    keys = jax.random.split(jax.random.fold_in(key, 11), 5)
    base = jnp.clip(jax.random.normal(keys[0], (RANK, NODES), jnp.float32), -5.0, 5.0)
    column = jnp.exp(jax.random.uniform(keys[1], (RANK,), jnp.float32, 0.0, 1.2))
    mixing = jnp.diag(column) + 0.4 * jax.random.normal(keys[2], (RANK, RANK), jnp.float32) / math.sqrt(RANK)
    position = jnp.arange(NODES, dtype=jnp.float32) / NODES
    rough = jnp.exp(jax.random.uniform(keys[4], (NODES,), jnp.float32, -0.35, 0.35))
    row_scale = 0.3 * jnp.sqrt(1.0 + 2.0 * position) * rough
    mixed = jnp.dot(mixing, base, precision=lax.Precision.HIGHEST) * row_scale[None, :]
    return jnp.clip(mixed, -12.0, 12.0)


def levels(key, shape, cuts, low, top_value):
    gain = 1.0
    for dim, parts in cuts:
        draws = jax.random.uniform(jax.random.fold_in(jax.random.fold_in(key, 6), dim), (parts,), jnp.float32, low / len(cuts), top_value / len(cuts))
        gain = gain * jnp.repeat(jnp.exp(draws), shape[dim] // parts).reshape((-1,) + (1,) * (len(shape) - 1 - dim))
    return gain


def gaussian(own_key, shape, width, most, cuts=(), kind=jnp.bfloat16):
    level = levels(own_key, shape, cuts, -0.22, 0.18) if cuts else 1.0
    array = jax.random.normal(own_key, shape, jnp.float32) * width * level
    return jnp.minimum(jnp.maximum(array, -most), most).astype(kind)


def setup_inputs(seed: int = 0) -> dict:
    arg_keys = jax.random.split(jax.random.key(seed), 4)
    return {
        "snapshots": gaussian(arg_keys[0], (PARAMS, TIMES, NODES), 1.0, 6.0, ((0, 2), (2, 128))),
        "space_start": draw_space_start(jax.random.fold_in(arg_keys[3], 71), 0),
        "time_start": gaussian(arg_keys[2], (RANK, TIMES), 0.15, 0.9, (), jnp.float32),
    }


ridge_share = 0.01

def gram_of(factor):
    return jnp.dot(factor, factor.T, precision=lax.Precision.HIGHEST)

def solve_gram(gram, right_side):
    count = gram.shape[0]
    ridge_term = ridge_share * jnp.trace(gram) / count
    matrix = gram + ridge_term * jnp.eye(count, dtype=gram.dtype)
    chol_factor = jnp.linalg.cholesky(matrix)
    return jax.scipy.linalg.cho_solve((chol_factor, True), right_side)

def reference(snapshots, space_start, time_start):
    samples, steps_count, node_count = snapshots.shape
    columns = space_start.shape[0]
    unfolded = snapshots.reshape(samples * steps_count, node_count)
    space_factor = space_start
    time_factor = time_start
    param_factor = None
    for sweep_index in range(SWEEPS):
        space_low = space_factor.astype(jnp.bfloat16)
        contracted = jnp.dot(unfolded.astype(jnp.float32), space_low.T.astype(jnp.float32), preferred_element_type=jnp.float32).reshape(samples, steps_count, columns)
        space_gram = gram_of(space_factor)
        param_side = jnp.einsum('jkr,rk->rj', contracted, time_factor, precision=lax.Precision.HIGHEST)
        param_factor = solve_gram(space_gram * gram_of(time_factor), param_side)
        param_gram = gram_of(param_factor)
        time_side = jnp.einsum('jkr,rj->rk', contracted, param_factor, precision=lax.Precision.HIGHEST)
        time_factor = solve_gram(space_gram * param_gram, time_side)
        khatri = (param_factor[:, :, None] * time_factor[:, None, :]).astype(jnp.bfloat16).reshape(columns, samples * steps_count)
        space_side = jnp.dot(khatri.astype(jnp.float32), unfolded.astype(jnp.float32), preferred_element_type=jnp.float32)
        space_factor = solve_gram(param_gram * gram_of(time_factor), space_side)
    return (space_factor, param_factor, time_factor)
```

```python
import functools

import jax
import jax.numpy as jnp
from jax import lax
from jax.experimental import pallas as pl
from jax.experimental.pallas import tpu as pltpu
from jax.sharding import Mesh
from jax.sharding import PartitionSpec as P

SWEEPS = 4
NODES = ("nodes_0", "nodes_1", "nodes_2")
PLANE = ("nodes_0", "nodes_2")
LINE = "nodes_1"
CORE = "params"
F32 = jnp.float32
BF16 = jnp.bfloat16
EXACT = lax.Precision.HIGHEST
RIDGE_SHARE = 0.01


def dot(a, b, over, precision=None):
    return lax.dot_general(
        a, b, (((over[0],), (over[1],)), ((), ())), precision=precision, preferred_element_type=F32
    )


def gram_rows(a):
    return dot(a, a, (0, 0), EXACT)


def row_of(x, i):
    return jnp.broadcast_to(x[i : i + 1, :], (8, x.shape[1]))


def column_of(x, i):
    return jnp.broadcast_to(x[:, i : i + 1], x.shape)


def eliminate(blocks):
    blocks = list(blocks)
    count = len(blocks)
    sub = lax.broadcasted_iota(jnp.int32, blocks[0].shape, 0)
    for k in range(count):
        lead = [column_of(blocks[k], 8 * k + i) for i in range(8)]
        others = {m: [column_of(blocks[m], 8 * k + i) for i in range(8)] for m in range(count) if m != k}
        rows = blocks[k]
        for i in range(8):
            pivot = sub == i
            factor = jnp.where(pivot, -1.0, lead[i]) * (1.0 / row_of(lead[i], i))
            rows = jnp.where(pivot, 0.0, rows) - factor * row_of(rows, i)
            for n in range(i + 1, 8):
                lead[n] = jnp.where(pivot, 0.0, lead[n]) - factor * row_of(lead[n], i)
        pivots = [row_of(rows, i) for i in range(8)]
        blocks[k] = rows
        for m, columns in others.items():
            terms = [columns[i] * pivots[i] for i in range(8)]
            while len(terms) > 1:
                terms = [terms[i] + terms[i + 1] for i in range(0, len(terms), 2)]
            blocks[m] = blocks[m] - terms[0]
    return blocks


def ridge_inverse(gram):
    n = gram.shape[0]
    row = lax.broadcasted_iota(jnp.int32, (n, n), 0)
    column = lax.broadcasted_iota(jnp.int32, (n, n), 1)
    eye = jnp.where(row == column, 1.0, 0.0).astype(F32)
    matrix = gram + (RIDGE_SHARE / n) * jnp.sum(gram * eye) * eye
    both = jnp.concatenate([matrix, eye], axis=1)
    done = eliminate([both[8 * m : 8 * m + 8, :] for m in range(n // 8)])
    return jnp.concatenate(done, axis=0)[:, n:]


def fold(x):
    half = x.shape[0] // 2
    return jnp.concatenate([x[:half, :], x[half:, :]], axis=1)


def unfold(x):
    half = x.shape[1] // 2
    return jnp.concatenate([x[:, :half], x[:, half:]], axis=0)


def total(parts):
    whole = [parts[i] for i in range(parts.shape[0])]
    while len(whole) > 1:
        whole = [whole[i] + whole[i + 1] for i in range(0, len(whole), 2)]
    return whole[0]


def contract(rows_ref, space, times_ref, contracted_ref, message_ref):
    rank = space.shape[0]
    steps = times_ref.shape[0]
    samples = message_ref.shape[0]
    low = space.astype(BF16)
    message_ref[:, rank:] = dot(space, space, (1, 1), EXACT)
    times = times_ref[...]
    group = 8
    for first in range(0, samples, group):
        part = dot(rows_ref[first * steps : (first + group) * steps, :], low, (1, 1))
        contracted_ref[first * steps : (first + group) * steps, :] = part
        sides = [
            jnp.sum(part[j * steps : (j + 1) * steps, :] * times, axis=0, keepdims=True) for j in range(group)
        ]
        message_ref[first : first + group, :rank] = jnp.concatenate(sides, axis=0)


def start_kernel(rows_ref, space_ref, times_ref, contracted_ref, message_ref):
    contract(rows_ref, space_ref[...], times_ref, contracted_ref, message_ref)


def space_kernel(rows_ref, own_ref, other_ref, inverse_ref, times_ref, space_ref, contracted_ref, message_ref):
    space = dot(inverse_ref[...], own_ref[...] + other_ref[...], (1, 0), EXACT)
    space_ref[...] = space
    contract(rows_ref, space, times_ref, contracted_ref, message_ref)


def last_kernel(own_ref, other_ref, inverse_ref, space_ref):
    space_ref[...] = dot(inverse_ref[...], own_ref[...] + other_ref[...], (1, 0), EXACT)


def params_kernel(parts_ref, times_ref, contracted_ref, params_ref, message_ref, space_gram_ref):
    steps, rank = times_ref.shape
    samples = params_ref.shape[0]
    whole = total(parts_ref)
    side, space_gram = whole[:, :rank], whole[:, rank:]
    space_gram_ref[...] = space_gram
    inverse = ridge_inverse(space_gram * gram_rows(times_ref[...]))
    params = dot(side, inverse, (1, 0), EXACT)
    params_ref[...] = params
    sums = [jnp.zeros((8, rank), F32) for _ in range(steps // 8)]
    for j in range(samples):
        factor = jnp.broadcast_to(params_ref[j : j + 1, :], (8, rank))
        for q in range(steps // 8):
            sums[q] = sums[q] + contracted_ref[j * steps + 8 * q : j * steps + 8 * q + 8, :] * factor
    message_ref[: steps // 2, :] = fold(jnp.concatenate(sums, axis=0))
    message_ref[steps // 2 :, :] = fold(gram_rows(params))


def inverse_kernel(first_ref, second_ref, inverse_ref):
    inverse_ref[...] = ridge_inverse(unfold(first_ref[...]) * second_ref[...])


def times_kernel(rows_ref, parts_ref, inverse_ref, params_ref, times_ref, gram_ref, side_ref, khatri_ref):
    steps, rank = times_ref.shape
    samples = params_ref.shape[0]
    times = dot(unfold(total(parts_ref)), inverse_ref[...], (1, 0), EXACT)
    times_ref[...] = times
    gram_ref[...] = gram_rows(times)
    for j in range(samples):
        factor = jnp.broadcast_to(params_ref[j : j + 1, :], times.shape)
        khatri_ref[j * steps : (j + 1) * steps, :] = (times * factor).astype(BF16)
    side_ref[...] = dot(khatri_ref[...], rows_ref[...], (0, 0))


def on_device(kernel, shapes, inputs, scratch=()):
    whole = pl.BlockSpec(memory_space=pltpu.VMEM)
    return pl.pallas_call(
        kernel,
        out_shape=[jax.ShapeDtypeStruct(shape, F32) for shape in shapes],
        in_specs=[whole] * inputs,
        out_specs=[whole] * len(shapes),
        scratch_shapes=list(scratch),
        compiler_params=pltpu.CompilerParams(vmem_limit_bytes=24 << 20),
    )


def copies(x, axes):
    everywhere = jnp.broadcast_to(x, (lax.axis_size(axes), *x.shape))
    return lax.all_to_all(everywhere, axes, split_axis=0, concat_axis=0, tiled=True)


def parts_of_nodes(x):
    return copies(jnp.sum(copies(x, PLANE), axis=0), LINE)


def other_core(x):
    return lax.ppermute(x, CORE, [(0, 1), (1, 0)])


def per_device(snapshots, space_start, time_start):
    samples, steps, nodes = snapshots.shape
    rank = space_start.shape[0]
    rows = snapshots.reshape(samples * steps, nodes)
    times = time_start.T
    start = on_device(start_kernel, [(samples * steps, rank), (samples, 2 * rank)], 3)
    again = on_device(space_kernel, [(rank, nodes), (samples * steps, rank), (samples, 2 * rank)], 5)
    last = on_device(last_kernel, [(rank, nodes)], 3)
    for_params = on_device(params_kernel, [(samples, rank), ((steps + rank) // 2, 2 * rank), (rank, rank)], 3)
    invert = on_device(inverse_kernel, [(rank, rank)], 2)
    for_times = on_device(
        times_kernel,
        [(steps, rank), (rank, rank), (rank, nodes)],
        4,
        [pltpu.VMEM((samples * steps, rank), BF16)],
    )
    contracted, message = start(rows, space_start, times)
    for sweep in range(SWEEPS):
        params, message, space_gram = for_params(parts_of_nodes(message), times, contracted)
        message = message + other_core(message)
        parts = parts_of_nodes(message[: steps // 2])
        param_gram = message[steps // 2 :]
        (inverse,) = invert(param_gram, space_gram)
        times, time_gram, side = for_times(rows, parts, inverse, params)
        (inverse,) = invert(param_gram, time_gram)
        other = other_core(side)
        if sweep + 1 < SWEEPS:
            space, contracted, message = again(rows, side, other, inverse, times)
        else:
            (space,) = last(side, other, inverse)
    return space, params.T, times.T


def solution(mesh):
    split = Mesh(
        mesh.devices.reshape(4, 8, 4, mesh.shape["params"]),
        ("nodes_0", "nodes_1", "nodes_2", "params"),
    )
    return jax.shard_map(
        per_device,
        mesh=split,
        in_specs=(P("params", None, NODES), P(None, NODES), P()),
        out_specs=(P(None, NODES), P(None, "params"), P()),
        check_vma=False,
    )
```

```python
import functools

import jax
import jax.numpy as jnp
from jax import lax
from jax.experimental import pallas as pl
from jax.experimental.pallas import tpu as pltpu
from jax.sharding import Mesh
from jax.sharding import PartitionSpec as P

SWEEPS = 4
NODES = ("nodes_0", "nodes_1", "nodes_2")
PLANE = ("nodes_0", "nodes_2")
LINE = "nodes_1"
CORE = "params"
GROUP = 8
F32 = jnp.float32
BF16 = jnp.bfloat16
EXACT = lax.Precision.HIGHEST
RIDGE_SHARE = 0.01


def dot(a, b, over, precision=None):
    return lax.dot_general(
        a, b, (((over[0],), (over[1],)), ((), ())), precision=precision, preferred_element_type=F32
    )


def gram_rows(a):
    return dot(a, a, (0, 0), EXACT)


def row_of(x, i):
    return jnp.broadcast_to(x[i : i + 1, :], (8, x.shape[1]))


def column_of(x, i):
    return jnp.broadcast_to(x[:, i : i + 1], x.shape)


def eliminate(blocks):
    blocks = list(blocks)
    count = len(blocks)
    sub = lax.broadcasted_iota(jnp.int32, blocks[0].shape, 0)
    for k in range(count):
        lead = [column_of(blocks[k], 8 * k + i) for i in range(8)]
        others = {m: [column_of(blocks[m], 8 * k + i) for i in range(8)] for m in range(count) if m != k}
        rows = blocks[k]
        for i in range(8):
            pivot = sub == i
            factor = jnp.where(pivot, -1.0, lead[i]) * (1.0 / row_of(lead[i], i))
            rows = jnp.where(pivot, 0.0, rows) - factor * row_of(rows, i)
            for n in range(i + 1, 8):
                lead[n] = jnp.where(pivot, 0.0, lead[n]) - factor * row_of(lead[n], i)
        pivots = [row_of(rows, i) for i in range(8)]
        blocks[k] = rows
        for m, columns in others.items():
            terms = [columns[i] * pivots[i] for i in range(8)]
            while len(terms) > 1:
                terms = [terms[i] + terms[i + 1] for i in range(0, len(terms), 2)]
            blocks[m] = blocks[m] - terms[0]
    return blocks


def ridge_inverse(gram):
    n = gram.shape[0]
    row = lax.broadcasted_iota(jnp.int32, (n, n), 0)
    column = lax.broadcasted_iota(jnp.int32, (n, n), 1)
    eye = jnp.where(row == column, 1.0, 0.0).astype(F32)
    matrix = gram + (RIDGE_SHARE / n) * jnp.sum(gram * eye) * eye
    both = jnp.concatenate([matrix, eye], axis=1)
    done = eliminate([both[8 * m : 8 * m + 8, :] for m in range(n // 8)])
    return jnp.concatenate(done, axis=0)[:, n:]


def fold(x):
    half = x.shape[0] // 2
    return jnp.concatenate([x[:half, :], x[half:, :]], axis=1)


def unfold(x):
    half = x.shape[1] // 2
    return jnp.concatenate([x[:, :half], x[:, half:]], axis=0)


def total(parts):
    whole = [parts[i] for i in range(parts.shape[0])]
    while len(whole) > 1:
        whole = [whole[i] + whole[i + 1] for i in range(0, len(whole), 2)]
    return whole[0]


def spread(ref, x, rows=slice(None)):
    for i in range(ref.shape[0]):
        ref[i, rows, :] = x


def contract(rows_of, space, times, samples, contracted_ref, message_ref):
    steps, rank = times.shape
    low = space.astype(BF16)
    spread(message_ref, fold(dot(space, space, (1, 1), EXACT)), slice(samples // 2, None))
    half = []
    for group in range(samples // GROUP):
        here = slice(group * GROUP * steps, (group + 1) * GROUP * steps)
        part = dot(rows_of(group), low, (1, 1))
        contracted_ref[here, :] = part
        sides = [
            jnp.sum(part[j * steps : (j + 1) * steps, :] * times, axis=0, keepdims=True) for j in range(GROUP)
        ]
        half.append(jnp.concatenate(sides, axis=0))
    spread(message_ref, fold(jnp.concatenate(half, axis=0)), slice(0, samples // 2))


def start_kernel(
    source_ref, space_ref, times_ref, rows_ref, contracted_ref, message_ref, space_here, times_here, arrived, early
):
    samples = rows_ref.shape[0] // times_ref.shape[0]
    size = rows_ref.shape[0] // (samples // GROUP)
    others = [
        pltpu.make_async_copy(space_ref, space_here, early.at[0]),
        pltpu.make_async_copy(times_ref, times_here, early.at[1]),
    ]
    for copy in others:
        copy.start()
    loads = [
        pltpu.make_async_copy(
            source_ref.at[i * size : (i + 1) * size, :], rows_ref.at[i * size : (i + 1) * size, :], arrived.at[i]
        )
        for i in range(samples // GROUP)
    ]
    for copy in loads:
        copy.start()
    for copy in others:
        copy.wait()

    def rows_of(group):
        loads[group].wait()
        return rows_ref[group * size : (group + 1) * size, :]

    contract(rows_of, space_here[...], times_here[...], samples, contracted_ref, message_ref)


def space_kernel(rows_ref, own_ref, other_ref, inverse_ref, times_ref, contracted_ref, message_ref):
    space = dot(inverse_ref[...], own_ref[...] + other_ref[...], (1, 0), EXACT)
    steps = times_ref.shape[0]
    size = GROUP * steps
    contract(
        lambda group: rows_ref[group * size : (group + 1) * size, :],
        space,
        times_ref[...],
        rows_ref.shape[0] // steps,
        contracted_ref,
        message_ref,
    )


def last_kernel(own_ref, other_ref, inverse_ref, space_ref):
    space_ref[...] = dot(inverse_ref[...], own_ref[...] + other_ref[...], (1, 0), EXACT)


def relay_kernel(parts_ref, copies_ref):
    spread(copies_ref, total(parts_ref))


def pair_kernel(own_ref, other_ref, copies_ref):
    spread(copies_ref, own_ref[...] + other_ref[...])


def params_kernel(parts_ref, times_ref, params_ref, gram_ref, space_gram_ref):
    half = params_ref.shape[0] // 2
    whole = total(parts_ref)
    side, space_gram = unfold(whole[:half, :]), unfold(whole[half:, :])
    space_gram_ref[...] = space_gram
    inverse = ridge_inverse(space_gram * gram_rows(times_ref[...]))
    params = dot(side, inverse, (1, 0), EXACT)
    params_ref[...] = params
    gram_ref[...] = fold(gram_rows(params))


def time_side_kernel(contracted_ref, params_ref, side_ref):
    samples, rank = params_ref.shape
    steps = 2 * side_ref.shape[0]
    sums = [jnp.zeros((8, rank), F32) for _ in range(steps // 8)]
    for j in range(samples):
        factor = jnp.broadcast_to(params_ref[j : j + 1, :], (8, rank))
        for q in range(steps // 8):
            sums[q] = sums[q] + contracted_ref[j * steps + 8 * q : j * steps + 8 * q + 8, :] * factor
    side_ref[...] = fold(jnp.concatenate(sums, axis=0))


def times_inverse_kernel(own_ref, other_ref, space_gram_ref, inverse_ref, gram_ref):
    gram = unfold(own_ref[...] + other_ref[...])
    gram_ref[...] = gram
    inverse_ref[...] = ridge_inverse(gram * space_gram_ref[...])


def space_inverse_kernel(first_ref, second_ref, inverse_ref):
    inverse_ref[...] = ridge_inverse(first_ref[...] * second_ref[...])


def times_kernel(rows_ref, parts_ref, inverse_ref, params_ref, times_ref, gram_ref, side_ref, khatri_ref):
    steps, rank = times_ref.shape
    samples = params_ref.shape[0]
    times = dot(unfold(total(parts_ref)), inverse_ref[...], (1, 0), EXACT)
    times_ref[...] = times
    gram_ref[...] = gram_rows(times)
    for j in range(samples):
        factor = jnp.broadcast_to(params_ref[j : j + 1, :], times.shape)
        khatri_ref[j * steps : (j + 1) * steps, :] = (times * factor).astype(BF16)
    side_ref[...] = dot(khatri_ref[...], rows_ref[...], (0, 0))


HERE = pl.BlockSpec(memory_space=pltpu.VMEM)
AWAY = pl.BlockSpec(memory_space=pltpu.HBM)


def on_device(kernel, shapes, inputs, scratch=(), limit=8):
    return pl.pallas_call(
        kernel,
        out_shape=[s if isinstance(s, jax.ShapeDtypeStruct) else jax.ShapeDtypeStruct(s, F32) for s in shapes],
        in_specs=[HERE] * inputs if isinstance(inputs, int) else inputs,
        out_specs=[HERE] * len(shapes),
        scratch_shapes=list(scratch),
        compiler_params=pltpu.CompilerParams(vmem_limit_bytes=limit << 20),
    )


def exchange(copies, axes):
    return lax.all_to_all(copies, axes, split_axis=0, concat_axis=0, tiled=True)


def other_core(x):
    return lax.ppermute(x, CORE, [(0, 1), (1, 0)])


def per_device(snapshots, space_start, time_start):
    samples, steps, nodes = snapshots.shape
    rank = space_start.shape[0]
    plane, line = lax.axis_size(PLANE), lax.axis_size(LINE)
    width = 2 * rank
    both = (samples + rank) // 2
    count = samples * steps
    source = snapshots.reshape(count, nodes)
    times = time_start.T
    rows_shape = jax.ShapeDtypeStruct((count, nodes), BF16)
    start = on_device(
        start_kernel,
        [rows_shape, (count, rank), (plane, both, width)],
        [AWAY, AWAY, AWAY],
        [
            pltpu.VMEM((rank, nodes), F32),
            pltpu.VMEM((steps, rank), F32),
            pltpu.SemaphoreType.DMA((samples // GROUP,)),
            pltpu.SemaphoreType.DMA((2,)),
        ],
        24,
    )
    again = on_device(space_kernel, [(count, rank), (plane, both, width)], 5, (), 24)
    last = on_device(last_kernel, [(rank, nodes)], 3)
    relay_both = on_device(relay_kernel, [(line, both, width)], 1)
    relay_times = on_device(relay_kernel, [(line, steps // 2, width)], 1)
    pair = on_device(pair_kernel, [(plane, steps // 2, width)], 2)
    for_params = on_device(params_kernel, [(samples, rank), (rank // 2, width), (rank, rank)], 2)
    time_side = on_device(time_side_kernel, [(steps // 2, width)], 2)
    times_inverse = on_device(times_inverse_kernel, [(rank, rank), (rank, rank)], 3)
    space_inverse = on_device(space_inverse_kernel, [(rank, rank)], 2)
    for_times = on_device(
        times_kernel, [(steps, rank), (rank, rank), (rank, nodes)], 4, [pltpu.VMEM((count, rank), BF16)], 24
    )
    away = [pltpu.with_memory_space_constraint(x, pltpu.HBM) for x in (source, space_start, times)]
    rows, contracted, message = start(*away)
    for sweep in range(SWEEPS):
        (message,) = relay_both(exchange(message, PLANE))
        params, gram, space_gram = for_params(exchange(message, LINE), times)
        other_gram = other_core(gram)
        (side,) = time_side(contracted, params)
        other_side = other_core(side)
        inverse, param_gram = times_inverse(gram, other_gram, space_gram)
        side, other_side, inverse = lax.optimization_barrier((side, other_side, inverse))
        (message,) = pair(side, other_side)
        (message,) = relay_times(exchange(message, PLANE))
        times, time_gram, side = for_times(rows, exchange(message, LINE), inverse, params)
        other = other_core(side)
        (inverse,) = space_inverse(param_gram, time_gram)
        if sweep + 1 < SWEEPS:
            contracted, message = again(rows, side, other, inverse, times)
        else:
            (space,) = last(side, other, inverse)
    return space, params.T, times.T


def solution(mesh):
    split = Mesh(
        mesh.devices.reshape(4, 8, 4, mesh.shape["params"]),
        ("nodes_0", "nodes_1", "nodes_2", "params"),
    )
    return jax.shard_map(
        per_device,
        mesh=split,
        in_specs=(P("params", None, NODES), P(None, NODES), P()),
        out_specs=(P(None, NODES), P(None, "params"), P()),
        check_vma=False,
    )
```

```python
import functools

import jax
import jax.numpy as jnp
from jax import lax
from jax.experimental import pallas as pl
from jax.experimental.pallas import tpu as pltpu
from jax.sharding import Mesh
from jax.sharding import PartitionSpec as P

SWEEPS = 4
NODES = ("nodes_0", "nodes_1", "nodes_2")
PLANE = ("nodes_0", "nodes_2")
LINE = "nodes_1"
CORE = "params"
GROUP = 8
GROUPS = 2
F32 = jnp.float32
BF16 = jnp.bfloat16
EXACT = lax.Precision.HIGHEST
RIDGE_SHARE = 0.01


def dot(a, b, over, precision=None):
    return lax.dot_general(
        a, b, (((over[0],), (over[1],)), ((), ())), precision=precision, preferred_element_type=F32
    )


def gram_rows(a):
    return dot(a, a, (0, 0), EXACT)


def row_of(x, i):
    return jnp.broadcast_to(x[i : i + 1, :], (8, x.shape[1]))


def column_of(x, i):
    return jnp.broadcast_to(x[:, i : i + 1], x.shape)


def eliminate(blocks):
    blocks = list(blocks)
    count = len(blocks)
    sub = lax.broadcasted_iota(jnp.int32, blocks[0].shape, 0)
    for k in range(count):
        lead = [column_of(blocks[k], 8 * k + i) for i in range(8)]
        others = {m: [column_of(blocks[m], 8 * k + i) for i in range(8)] for m in range(count) if m != k}
        rows = blocks[k]
        for i in range(8):
            pivot = sub == i
            factor = jnp.where(pivot, -1.0, lead[i]) * (1.0 / row_of(lead[i], i))
            rows = jnp.where(pivot, 0.0, rows) - factor * row_of(rows, i)
            for n in range(i + 1, 8):
                lead[n] = jnp.where(pivot, 0.0, lead[n]) - factor * row_of(lead[n], i)
        pivots = [row_of(rows, i) for i in range(8)]
        blocks[k] = rows
        for m, columns in others.items():
            terms = [columns[i] * pivots[i] for i in range(8)]
            while len(terms) > 1:
                terms = [terms[i] + terms[i + 1] for i in range(0, len(terms), 2)]
            blocks[m] = blocks[m] - terms[0]
    return blocks


def ridge_inverse(gram):
    n = gram.shape[0]
    row = lax.broadcasted_iota(jnp.int32, (n, n), 0)
    column = lax.broadcasted_iota(jnp.int32, (n, n), 1)
    eye = jnp.where(row == column, 1.0, 0.0).astype(F32)
    trace = jnp.sum(jnp.sum(gram * eye, axis=0, keepdims=True), axis=1, keepdims=True)
    matrix = gram + (RIDGE_SHARE / n) * trace * eye
    both = jnp.concatenate([matrix, eye], axis=1)
    done = eliminate([both[8 * m : 8 * m + 8, :] for m in range(n // 8)])
    return jnp.concatenate(done, axis=0)[:, n:]


def fold(x):
    half = x.shape[0] // 2
    return jnp.concatenate([x[:half, :], x[half:, :]], axis=1)


def unfold(x):
    half = x.shape[1] // 2
    return jnp.concatenate([x[:, :half], x[:, half:]], axis=0)


def total(parts):
    whole = [parts[i] for i in range(parts.shape[0])]
    while len(whole) > 1:
        whole = [whole[i] + whole[i + 1] for i in range(0, len(whole), 2)]
    return whole[0]


def spread(ref, x, rows=slice(None)):
    for i in range(ref.shape[0]):
        ref[i, rows, :] = x


def contract(rows_ref, space, times, contracted_ref, message_ref, side_ref, arrive=None):
    steps, rank = times.shape
    samples = side_ref.shape[0]
    low = space.astype(BF16)
    spread(message_ref, fold(dot(space, space, (1, 1), EXACT)), slice(samples // 2, None))

    def groups(step, carry):
        if arrive is not None:
            arrive(step)
        for group in range(GROUPS):
            first = pl.multiple_of((step * GROUPS + group) * GROUP, GROUP)
            here = pl.ds(pl.multiple_of(first * steps, GROUP * steps), GROUP * steps)
            part = dot(rows_ref[here, :], low, (1, 1))
            contracted_ref[here, :] = part
            sides = [
                jnp.sum(part[j * steps : (j + 1) * steps, :] * times, axis=0, keepdims=True) for j in range(GROUP)
            ]
            side_ref[pl.ds(first, GROUP), :] = jnp.concatenate(sides, axis=0)
        return carry

    lax.fori_loop(0, samples // (GROUP * GROUPS), groups, 0)
    spread(message_ref, fold(side_ref[...]), slice(0, samples // 2))


def start_kernel(
    source_ref, space_ref, times_ref, rows_ref, contracted_ref, message_ref, side_ref, space_here, times_here, arrived, early
):
    count = arrived.shape[0]
    size = rows_ref.shape[0] // count
    others = [
        pltpu.make_async_copy(space_ref, space_here, early.at[0]),
        pltpu.make_async_copy(times_ref, times_here, early.at[1]),
    ]
    for copy in others:
        copy.start()

    def load(i):
        here = pl.ds(pl.multiple_of(i * size, size), size)
        return pltpu.make_async_copy(source_ref.at[here, :], rows_ref.at[here, :], arrived.at[i])

    for i in range(count):
        load(i).start()
    for copy in others:
        copy.wait()
    contract(
        rows_ref, space_here[...], times_here[...], contracted_ref, message_ref, side_ref, lambda step: load(step).wait()
    )


def space_kernel(rows_ref, own_ref, other_ref, inverse_ref, times_ref, contracted_ref, message_ref, side_ref):
    space = dot(inverse_ref[...], own_ref[...] + other_ref[...], (1, 0), EXACT)
    contract(rows_ref, space, times_ref[...], contracted_ref, message_ref, side_ref)


def last_kernel(own_ref, other_ref, inverse_ref, space_ref):
    space_ref[...] = dot(inverse_ref[...], own_ref[...] + other_ref[...], (1, 0), EXACT)


def relay_kernel(parts_ref, copies_ref):
    spread(copies_ref, total(parts_ref))


def pair_kernel(own_ref, other_ref, copies_ref):
    spread(copies_ref, own_ref[...] + other_ref[...])


def params_kernel(parts_ref, times_ref, params_ref, gram_ref, space_gram_ref):
    half = params_ref.shape[0] // 2
    whole = total(parts_ref)
    side, space_gram = unfold(whole[:half, :]), unfold(whole[half:, :])
    space_gram_ref[...] = space_gram
    inverse = ridge_inverse(space_gram * gram_rows(times_ref[...]))
    params = dot(side, inverse, (1, 0), EXACT)
    params_ref[...] = params
    gram_ref[...] = fold(gram_rows(params))


def time_side_kernel(contracted_ref, params_ref, side_ref):
    samples, rank = params_ref.shape
    steps = 2 * side_ref.shape[0]
    sums = [jnp.zeros((8, rank), F32) for _ in range(steps // 8)]
    for j in range(samples):
        factor = jnp.broadcast_to(params_ref[j : j + 1, :], (8, rank))
        for q in range(steps // 8):
            sums[q] = sums[q] + contracted_ref[j * steps + 8 * q : j * steps + 8 * q + 8, :] * factor
    side_ref[...] = fold(jnp.concatenate(sums, axis=0))


def times_inverse_kernel(own_ref, other_ref, space_gram_ref, inverse_ref, gram_ref):
    gram = unfold(own_ref[...] + other_ref[...])
    gram_ref[...] = gram
    inverse_ref[...] = ridge_inverse(gram * space_gram_ref[...])


def space_inverse_kernel(first_ref, second_ref, inverse_ref):
    inverse_ref[...] = ridge_inverse(first_ref[...] * second_ref[...])


def times_kernel(rows_ref, parts_ref, inverse_ref, params_ref, times_ref, gram_ref, side_ref, khatri_ref):
    steps, rank = times_ref.shape
    samples = params_ref.shape[0]
    times = dot(unfold(total(parts_ref)), inverse_ref[...], (1, 0), EXACT)
    times_ref[...] = times
    gram_ref[...] = gram_rows(times)
    for j in range(samples):
        factor = jnp.broadcast_to(params_ref[j : j + 1, :], times.shape)
        khatri_ref[j * steps : (j + 1) * steps, :] = (times * factor).astype(BF16)
    side_ref[...] = dot(khatri_ref[...], rows_ref[...], (0, 0))


HERE = pl.BlockSpec(memory_space=pltpu.VMEM)
AWAY = pl.BlockSpec(memory_space=pltpu.HBM)


def on_device(kernel, shapes, inputs, scratch=(), limit=8):
    return pl.pallas_call(
        kernel,
        out_shape=[s if isinstance(s, jax.ShapeDtypeStruct) else jax.ShapeDtypeStruct(s, F32) for s in shapes],
        in_specs=[HERE] * inputs if isinstance(inputs, int) else inputs,
        out_specs=[HERE] * len(shapes),
        scratch_shapes=list(scratch),
        compiler_params=pltpu.CompilerParams(vmem_limit_bytes=limit << 20),
    )


def exchange(copies, axes):
    return lax.all_to_all(copies, axes, split_axis=0, concat_axis=0, tiled=True)


def other_core(x):
    return lax.ppermute(x, CORE, [(0, 1), (1, 0)])


def per_device(snapshots, space_start, time_start):
    samples, steps, nodes = snapshots.shape
    rank = space_start.shape[0]
    plane, line = lax.axis_size(PLANE), lax.axis_size(LINE)
    width = 2 * rank
    both = (samples + rank) // 2
    count = samples * steps
    source = snapshots.reshape(count, nodes)
    times = time_start.T
    rows_shape = jax.ShapeDtypeStruct((count, nodes), BF16)
    start = on_device(
        start_kernel,
        [rows_shape, (count, rank), (plane, both, width)],
        [AWAY, AWAY, AWAY],
        [
            pltpu.VMEM((samples, rank), F32),
            pltpu.VMEM((rank, nodes), F32),
            pltpu.VMEM((steps, rank), F32),
            pltpu.SemaphoreType.DMA((samples // (GROUP * GROUPS),)),
            pltpu.SemaphoreType.DMA((2,)),
        ],
        24,
    )
    again = on_device(
        space_kernel, [(count, rank), (plane, both, width)], 5, [pltpu.VMEM((samples, rank), F32)], 24
    )
    last = on_device(last_kernel, [(rank, nodes)], 3)
    relay_both = on_device(relay_kernel, [(line, both, width)], 1)
    relay_times = on_device(relay_kernel, [(line, steps // 2, width)], 1)
    pair = on_device(pair_kernel, [(plane, steps // 2, width)], 2)
    for_params = on_device(params_kernel, [(samples, rank), (rank // 2, width), (rank, rank)], 2)
    time_side = on_device(time_side_kernel, [(steps // 2, width)], 2)
    times_inverse = on_device(times_inverse_kernel, [(rank, rank), (rank, rank)], 3)
    space_inverse = on_device(space_inverse_kernel, [(rank, rank)], 2)
    for_times = on_device(
        times_kernel, [(steps, rank), (rank, rank), (rank, nodes)], 4, [pltpu.VMEM((count, rank), BF16)], 24
    )
    away = [pltpu.with_memory_space_constraint(x, pltpu.HBM) for x in (source, space_start, times)]
    rows, contracted, message = start(*away)
    for sweep in range(SWEEPS):
        (message,) = relay_both(exchange(message, PLANE))
        params, gram, space_gram = for_params(exchange(message, LINE), times)
        other_gram = other_core(gram)
        (side,) = time_side(contracted, params)
        other_side = other_core(side)
        inverse, param_gram = times_inverse(gram, other_gram, space_gram)
        side, other_side, inverse = lax.optimization_barrier((side, other_side, inverse))
        (message,) = pair(side, other_side)
        (message,) = relay_times(exchange(message, PLANE))
        times, time_gram, side = for_times(rows, exchange(message, LINE), inverse, params)
        other = other_core(side)
        (inverse,) = space_inverse(param_gram, time_gram)
        if sweep + 1 < SWEEPS:
            contracted, message = again(rows, side, other, inverse, times)
        else:
            (space,) = last(side, other, inverse)
    return space, params.T, times.T


def solution(mesh):
    split = Mesh(
        mesh.devices.reshape(4, 8, 4, mesh.shape["params"]),
        ("nodes_0", "nodes_1", "nodes_2", "params"),
    )
    return jax.shard_map(
        per_device,
        mesh=split,
        in_specs=(P("params", None, NODES), P(None, NODES), P()),
        out_specs=(P(None, NODES), P(None, "params"), P()),
        check_vma=False,
    )
```

```python
import functools

import jax
import jax.numpy as jnp
from jax import lax
from jax.experimental import pallas as pl
from jax.experimental.pallas import tpu as pltpu
from jax.sharding import Mesh
from jax.sharding import PartitionSpec as P

SWEEPS = 4
NODES = ("nodes_0", "nodes_1", "nodes_2")
PLANE = ("nodes_0", "nodes_2")
LINE = "nodes_1"
CORE = "params"
GROUP = 8
GROUPS = 2
F32 = jnp.float32
BF16 = jnp.bfloat16
EXACT = lax.Precision.HIGHEST
RIDGE_SHARE = 0.01


def dot(a, b, over, precision=None):
    return lax.dot_general(
        a, b, (((over[0],), (over[1],)), ((), ())), precision=precision, preferred_element_type=F32
    )


def gram_rows(a):
    return dot(a, a, (0, 0), EXACT)


def row_of(x, i):
    return jnp.broadcast_to(x[i : i + 1, :], (8, x.shape[1]))


def column_of(x, i):
    return jnp.broadcast_to(x[:, i : i + 1], x.shape)


def eliminate(blocks):
    blocks = list(blocks)
    count = len(blocks)
    sub = lax.broadcasted_iota(jnp.int32, blocks[0].shape, 0)
    for k in range(count):
        lead = [column_of(blocks[k], 8 * k + i) for i in range(8)]
        others = {m: [column_of(blocks[m], 8 * k + i) for i in range(8)] for m in range(count) if m != k}
        rows = blocks[k]
        for i in range(8):
            pivot = sub == i
            factor = jnp.where(pivot, -1.0, lead[i]) * (1.0 / row_of(lead[i], i))
            rows = jnp.where(pivot, 0.0, rows) - factor * row_of(rows, i)
            for n in range(i + 1, 8):
                lead[n] = jnp.where(pivot, 0.0, lead[n]) - factor * row_of(lead[n], i)
        pivots = [row_of(rows, i) for i in range(8)]
        blocks[k] = rows
        for m, columns in others.items():
            terms = [columns[i] * pivots[i] for i in range(8)]
            while len(terms) > 1:
                terms = [terms[i] + terms[i + 1] for i in range(0, len(terms), 2)]
            blocks[m] = blocks[m] - terms[0]
    return blocks


def ridge_inverse(gram):
    n = gram.shape[0]
    row = lax.broadcasted_iota(jnp.int32, (n, n), 0)
    column = lax.broadcasted_iota(jnp.int32, (n, n), 1)
    eye = jnp.where(row == column, 1.0, 0.0).astype(F32)
    trace = jnp.sum(jnp.sum(gram * eye, axis=0, keepdims=True), axis=1, keepdims=True)
    matrix = gram + (RIDGE_SHARE / n) * trace * eye
    both = jnp.concatenate([matrix, eye], axis=1)
    done = eliminate([both[8 * m : 8 * m + 8, :] for m in range(n // 8)])
    return jnp.concatenate(done, axis=0)[:, n:]


def fold(x):
    half = x.shape[0] // 2
    return jnp.concatenate([x[:half, :], x[half:, :]], axis=1)


def unfold(x):
    half = x.shape[1] // 2
    return jnp.concatenate([x[:, :half], x[:, half:]], axis=0)


def pack(gram):
    half = gram.shape[0] // 2
    row = lax.broadcasted_iota(jnp.int32, (half, half), 0)
    column = lax.broadcasted_iota(jnp.int32, (half, half), 1)
    first, cross, last = gram[:half, :half], gram[:half, half:], gram[half:, half:]
    body = fold(jnp.concatenate([jnp.where(row <= column, first, last), cross], axis=1))
    diagonal = jnp.sum(jnp.where(row == column, last, 0.0), axis=0, keepdims=True)
    blank = jnp.zeros((1, body.shape[1] - half), F32)
    return body, jnp.concatenate([diagonal, blank], axis=1)


def unpack(body, tail):
    body = unfold(body)
    half = body.shape[0]
    row = lax.broadcasted_iota(jnp.int32, (half, half), 0)
    column = lax.broadcasted_iota(jnp.int32, (half, half), 1)
    mixed, cross = body[:, :half], body[:, half:]
    turned = mixed.T
    first = jnp.where(row <= column, mixed, turned)
    diagonal = jnp.broadcast_to(tail[:, :half], (half, half))
    last = jnp.where(row > column, mixed, jnp.where(row < column, turned, diagonal))
    return jnp.concatenate(
        [jnp.concatenate([first, cross], axis=1), jnp.concatenate([cross.T, last], axis=1)], axis=0
    )


def total(parts):
    whole = [parts[i] for i in range(parts.shape[0])]
    while len(whole) > 1:
        whole = [whole[i] + whole[i + 1] for i in range(0, len(whole), 2)]
    return whole[0]


def spread(ref, x, rows=slice(None)):
    for i in range(ref.shape[0]):
        ref[i, rows, :] = x


def contract(rows_ref, space, times, contracted_ref, message_ref, side_ref, arrive=None):
    steps, rank = times.shape
    samples = side_ref.shape[0]
    low = space.astype(BF16)
    body, tail = pack(dot(space, space, (1, 1), EXACT))
    split = samples // 2 + rank // 4
    spread(message_ref, body, slice(samples // 2, split))
    spread(message_ref, tail, slice(split, split + 1))

    def groups(step, carry):
        if arrive is not None:
            arrive(step)
        for group in range(GROUPS):
            first = pl.multiple_of((step * GROUPS + group) * GROUP, GROUP)
            here = pl.ds(pl.multiple_of(first * steps, GROUP * steps), GROUP * steps)
            part = dot(rows_ref[here, :], low, (1, 1))
            contracted_ref[here, :] = part
            sides = [
                jnp.sum(part[j * steps : (j + 1) * steps, :] * times, axis=0, keepdims=True) for j in range(GROUP)
            ]
            side_ref[pl.ds(first, GROUP), :] = jnp.concatenate(sides, axis=0)
        return carry

    lax.fori_loop(0, samples // (GROUP * GROUPS), groups, 0)
    spread(message_ref, fold(side_ref[...]), slice(0, samples // 2))


def start_kernel(
    source_ref,
    space_ref,
    times_ref,
    rows_ref,
    contracted_ref,
    message_ref,
    gram_ref,
    side_ref,
    space_here,
    times_here,
    arrived,
    early,
):
    count = arrived.shape[0]
    size = rows_ref.shape[0] // count
    others = [
        pltpu.make_async_copy(space_ref, space_here, early.at[0]),
        pltpu.make_async_copy(times_ref, times_here, early.at[1]),
    ]
    for copy in others:
        copy.start()

    def load(i):
        here = pl.ds(pl.multiple_of(i * size, size), size)
        return pltpu.make_async_copy(source_ref.at[here, :], rows_ref.at[here, :], arrived.at[i])

    for i in range(count):
        load(i).start()
    for copy in others:
        copy.wait()
    gram_ref[...] = gram_rows(times_here[...])
    contract(
        rows_ref, space_here[...], times_here[...], contracted_ref, message_ref, side_ref, lambda step: load(step).wait()
    )


def space_kernel(rows_ref, own_ref, other_ref, inverse_ref, times_ref, contracted_ref, message_ref, side_ref):
    space = dot(inverse_ref[...], own_ref[...] + other_ref[...], (1, 0), EXACT)
    contract(rows_ref, space, times_ref[...], contracted_ref, message_ref, side_ref)


def last_kernel(own_ref, other_ref, inverse_ref, space_ref):
    space_ref[...] = dot(inverse_ref[...], own_ref[...] + other_ref[...], (1, 0), EXACT)


def relay_kernel(parts_ref, copies_ref):
    spread(copies_ref, total(parts_ref))


def pair_kernel(own_ref, other_ref, copies_ref):
    spread(copies_ref, own_ref[...] + other_ref[...])


def params_kernel(parts_ref, time_gram_ref, params_ref, gram_ref, space_gram_ref):
    half = params_ref.shape[0] // 2
    whole = total(parts_ref)
    split = whole.shape[0] - 1
    side, space_gram = unfold(whole[:half, :]), unpack(whole[half:split, :], whole[split:, :])
    space_gram_ref[...] = space_gram
    inverse = ridge_inverse(space_gram * time_gram_ref[...])
    params = dot(side, inverse, (1, 0), EXACT)
    params_ref[...] = params
    gram_ref[...] = fold(gram_rows(params))


def time_side_kernel(contracted_ref, params_ref, side_ref):
    samples, rank = params_ref.shape
    steps = 2 * side_ref.shape[0]
    sums = [jnp.zeros((8, rank), F32) for _ in range(steps // 8)]
    for j in range(samples):
        factor = jnp.broadcast_to(params_ref[j : j + 1, :], (8, rank))
        for q in range(steps // 8):
            sums[q] = sums[q] + contracted_ref[j * steps + 8 * q : j * steps + 8 * q + 8, :] * factor
    side_ref[...] = fold(jnp.concatenate(sums, axis=0))


def times_inverse_kernel(own_ref, other_ref, space_gram_ref, inverse_ref, gram_ref):
    gram = unfold(own_ref[...] + other_ref[...])
    gram_ref[...] = gram
    inverse_ref[...] = ridge_inverse(gram * space_gram_ref[...])


def space_inverse_kernel(first_ref, second_ref, inverse_ref):
    inverse_ref[...] = ridge_inverse(first_ref[...] * second_ref[...])


def times_kernel(rows_ref, parts_ref, inverse_ref, params_ref, times_ref, gram_ref, side_ref, khatri_ref):
    steps, rank = times_ref.shape
    samples = params_ref.shape[0]
    times = dot(unfold(total(parts_ref)), inverse_ref[...], (1, 0), EXACT)
    times_ref[...] = times
    gram_ref[...] = gram_rows(times)
    for j in range(samples):
        factor = jnp.broadcast_to(params_ref[j : j + 1, :], times.shape)
        khatri_ref[j * steps : (j + 1) * steps, :] = (times * factor).astype(BF16)
    side_ref[...] = dot(khatri_ref[...], rows_ref[...], (0, 0))


HERE = pl.BlockSpec(memory_space=pltpu.VMEM)
AWAY = pl.BlockSpec(memory_space=pltpu.HBM)


def on_device(kernel, shapes, inputs, scratch=(), limit=8):
    return pl.pallas_call(
        kernel,
        out_shape=[s if isinstance(s, jax.ShapeDtypeStruct) else jax.ShapeDtypeStruct(s, F32) for s in shapes],
        in_specs=[HERE] * inputs if isinstance(inputs, int) else inputs,
        out_specs=[HERE] * len(shapes),
        scratch_shapes=list(scratch),
        compiler_params=pltpu.CompilerParams(vmem_limit_bytes=limit << 20),
    )


def exchange(copies, axes):
    return lax.all_to_all(copies, axes, split_axis=0, concat_axis=0, tiled=True)


def other_core(x):
    return lax.ppermute(x, CORE, [(0, 1), (1, 0)])


def per_device(snapshots, space_start, time_start):
    samples, steps, nodes = snapshots.shape
    rank = space_start.shape[0]
    plane, line = lax.axis_size(PLANE), lax.axis_size(LINE)
    width = 2 * rank
    both = samples // 2 + rank // 4 + 1
    count = samples * steps
    source = snapshots.reshape(count, nodes)
    times = time_start.T
    rows_shape = jax.ShapeDtypeStruct((count, nodes), BF16)
    start = on_device(
        start_kernel,
        [rows_shape, (count, rank), (plane, both, width), (rank, rank)],
        [AWAY, AWAY, AWAY],
        [
            pltpu.VMEM((samples, rank), F32),
            pltpu.VMEM((rank, nodes), F32),
            pltpu.VMEM((steps, rank), F32),
            pltpu.SemaphoreType.DMA((samples // (GROUP * GROUPS),)),
            pltpu.SemaphoreType.DMA((2,)),
        ],
        24,
    )
    again = on_device(
        space_kernel, [(count, rank), (plane, both, width)], 5, [pltpu.VMEM((samples, rank), F32)], 24
    )
    last = on_device(last_kernel, [(rank, nodes)], 3)
    relay_both = on_device(relay_kernel, [(line, both, width)], 1)
    relay_times = on_device(relay_kernel, [(line, steps // 2, width)], 1)
    pair = on_device(pair_kernel, [(plane, steps // 2, width)], 2)
    for_params = on_device(params_kernel, [(samples, rank), (rank // 2, width), (rank, rank)], 2)
    time_side = on_device(time_side_kernel, [(steps // 2, width)], 2)
    times_inverse = on_device(times_inverse_kernel, [(rank, rank), (rank, rank)], 3)
    space_inverse = on_device(space_inverse_kernel, [(rank, rank)], 2)
    for_times = on_device(
        times_kernel, [(steps, rank), (rank, rank), (rank, nodes)], 4, [pltpu.VMEM((count, rank), BF16)], 24
    )
    away = [pltpu.with_memory_space_constraint(x, pltpu.HBM) for x in (source, space_start, times)]
    rows, contracted, message, time_gram = start(*away)
    for sweep in range(SWEEPS):
        (message,) = relay_both(exchange(message, PLANE))
        params, gram, space_gram = for_params(exchange(message, LINE), time_gram)
        other_gram = other_core(gram)
        (side,) = time_side(contracted, params)
        other_side = other_core(side)
        inverse, param_gram = times_inverse(gram, other_gram, space_gram)
        side, other_side, inverse = lax.optimization_barrier((side, other_side, inverse))
        (message,) = pair(side, other_side)
        (message,) = relay_times(exchange(message, PLANE))
        times, time_gram, side = for_times(rows, exchange(message, LINE), inverse, params)
        other = other_core(side)
        (inverse,) = space_inverse(param_gram, time_gram)
        if sweep + 1 < SWEEPS:
            contracted, message = again(rows, side, other, inverse, times)
        else:
            (space,) = last(side, other, inverse)
    return space, params.T, times.T


def solution(mesh):
    split = Mesh(
        mesh.devices.reshape(4, 8, 4, mesh.shape["params"]),
        ("nodes_0", "nodes_1", "nodes_2", "params"),
    )
    return jax.shard_map(
        per_device,
        mesh=split,
        in_specs=(P("params", None, NODES), P(None, NODES), P()),
        out_specs=(P(None, NODES), P(None, "params"), P()),
        check_vma=False,
    )
```

```python
import functools

import jax
import jax.numpy as jnp
from jax import lax
from jax.experimental import pallas as pl
from jax.experimental.pallas import tpu as pltpu
from jax.sharding import Mesh
from jax.sharding import PartitionSpec as P

SWEEPS = 4
NODES = ("nodes_0", "nodes_1", "nodes_2")
PLANE = ("nodes_0", "nodes_2")
LINE = "nodes_1"
CORE = "params"
GROUP = 8
CHUNK = 2
WHOLE = 8
F32 = jnp.float32
BF16 = jnp.bfloat16
EXACT = lax.Precision.HIGHEST
RIDGE_SHARE = 0.01


def dot(a, b, over, precision=None):
    return lax.dot_general(
        a, b, (((over[0],), (over[1],)), ((), ())), precision=precision, preferred_element_type=F32
    )


def gram_rows(a):
    return dot(a, a, (0, 0), EXACT)


def row_of(x, i):
    return jnp.broadcast_to(x[i : i + 1, :], (8, x.shape[1]))


def column_of(x, i):
    return jnp.broadcast_to(x[:, i : i + 1], x.shape)


def eliminate(blocks):
    blocks = list(blocks)
    count = len(blocks)
    sub = lax.broadcasted_iota(jnp.int32, blocks[0].shape, 0)
    for k in range(count):
        lead = [column_of(blocks[k], 8 * k + i) for i in range(8)]
        others = {m: [column_of(blocks[m], 8 * k + i) for i in range(8)] for m in range(count) if m != k}
        rows = blocks[k]
        for i in range(8):
            pivot = sub == i
            factor = jnp.where(pivot, -1.0, lead[i]) * (1.0 / row_of(lead[i], i))
            rows = jnp.where(pivot, 0.0, rows) - factor * row_of(rows, i)
            for n in range(i + 1, 8):
                lead[n] = jnp.where(pivot, 0.0, lead[n]) - factor * row_of(lead[n], i)
        pivots = [row_of(rows, i) for i in range(8)]
        blocks[k] = rows
        for m, columns in others.items():
            terms = [columns[i] * pivots[i] for i in range(8)]
            while len(terms) > 1:
                terms = [terms[i] + terms[i + 1] for i in range(0, len(terms), 2)]
            blocks[m] = blocks[m] - terms[0]
    return blocks


def ridge_inverse(gram):
    n = gram.shape[0]
    row = lax.broadcasted_iota(jnp.int32, (n, n), 0)
    column = lax.broadcasted_iota(jnp.int32, (n, n), 1)
    eye = jnp.where(row == column, 1.0, 0.0).astype(F32)
    trace = jnp.sum(jnp.sum(gram * eye, axis=0, keepdims=True), axis=1, keepdims=True)
    matrix = gram + (RIDGE_SHARE / n) * trace * eye
    both = jnp.concatenate([matrix, eye], axis=1)
    done = eliminate([both[8 * m : 8 * m + 8, :] for m in range(n // 8)])
    return jnp.concatenate(done, axis=0)[:, n:]


def fold(x):
    half = x.shape[0] // 2
    return jnp.concatenate([x[:half, :], x[half:, :]], axis=1)


def unfold(x):
    half = x.shape[1] // 2
    return jnp.concatenate([x[:, :half], x[:, half:]], axis=0)


def pack(gram):
    half = gram.shape[0] // 2
    row = lax.broadcasted_iota(jnp.int32, (half, half), 0)
    column = lax.broadcasted_iota(jnp.int32, (half, half), 1)
    first, cross, last = gram[:half, :half], gram[:half, half:], gram[half:, half:]
    body = fold(jnp.concatenate([jnp.where(row <= column, first, last), cross], axis=1))
    diagonal = jnp.sum(jnp.where(row == column, last, 0.0), axis=0, keepdims=True)
    blank = jnp.zeros((1, body.shape[1] - half), F32)
    return body, jnp.concatenate([diagonal, blank], axis=1)


def unpack(body, tail):
    body = unfold(body)
    half = body.shape[0]
    row = lax.broadcasted_iota(jnp.int32, (half, half), 0)
    column = lax.broadcasted_iota(jnp.int32, (half, half), 1)
    mixed, cross = body[:, :half], body[:, half:]
    turned = mixed.T
    first = jnp.where(row <= column, mixed, turned)
    diagonal = jnp.broadcast_to(tail[:, :half], (half, half))
    last = jnp.where(row > column, mixed, jnp.where(row < column, turned, diagonal))
    return jnp.concatenate(
        [jnp.concatenate([first, cross], axis=1), jnp.concatenate([cross.T, last], axis=1)], axis=0
    )


def total(parts):
    whole = [parts[i] for i in range(parts.shape[0])]
    while len(whole) > 1:
        whole = [whole[i] + whole[i + 1] for i in range(0, len(whole), 2)]
    return whole[0]


def spread(ref, x, rows=slice(None)):
    for i in range(ref.shape[0]):
        ref[i, rows, :] = x


def contract(rows_ref, space, times, contracted_ref, message_ref, side_ref, groups_at_once, arrive=None):
    steps, rank = times.shape
    samples = side_ref.shape[0]
    low = space.astype(BF16)
    body, tail = pack(dot(space, space, (1, 1), EXACT))
    split = samples // 2 + rank // 4
    spread(message_ref, body, slice(samples // 2, split))
    spread(message_ref, tail, slice(split, split + 1))

    def groups(step, carry):
        if arrive is not None:
            arrive(step)
        for group in range(groups_at_once):
            first = pl.multiple_of((step * groups_at_once + group) * GROUP, GROUP)
            here = pl.ds(pl.multiple_of(first * steps, GROUP * steps), GROUP * steps)
            part = dot(rows_ref[here, :], low, (1, 1))
            contracted_ref[here, :] = part
            sides = [
                jnp.sum(part[j * steps : (j + 1) * steps, :] * times, axis=0, keepdims=True) for j in range(GROUP)
            ]
            side_ref[pl.ds(first, GROUP), :] = jnp.concatenate(sides, axis=0)
        return carry

    lax.fori_loop(0, samples // (GROUP * groups_at_once), groups, 0)
    spread(message_ref, fold(side_ref[...]), slice(0, samples // 2))


def start_kernel(
    source_ref,
    space_ref,
    times_ref,
    rows_ref,
    contracted_ref,
    message_ref,
    gram_ref,
    side_ref,
    space_here,
    times_here,
    arrived,
    early,
):
    count = arrived.shape[0]
    size = rows_ref.shape[0] // count
    others = [
        pltpu.make_async_copy(space_ref, space_here, early.at[0]),
        pltpu.make_async_copy(times_ref, times_here, early.at[1]),
    ]
    for copy in others:
        copy.start()

    def load(i):
        here = pl.ds(pl.multiple_of(i * size, size), size)
        return pltpu.make_async_copy(source_ref.at[here, :], rows_ref.at[here, :], arrived.at[i])

    for i in range(count):
        load(i).start()
    for copy in others:
        copy.wait()
    gram_ref[...] = gram_rows(times_here[...])
    contract(
        rows_ref,
        space_here[...],
        times_here[...],
        contracted_ref,
        message_ref,
        side_ref,
        CHUNK,
        lambda step: load(step).wait(),
    )


def space_kernel(rows_ref, own_ref, other_ref, inverse_ref, times_ref, contracted_ref, message_ref, side_ref):
    space = dot(inverse_ref[...], own_ref[...] + other_ref[...], (1, 0), EXACT)
    contract(rows_ref, space, times_ref[...], contracted_ref, message_ref, side_ref, WHOLE)


def last_kernel(own_ref, other_ref, inverse_ref, space_ref):
    space_ref[...] = dot(inverse_ref[...], own_ref[...] + other_ref[...], (1, 0), EXACT)


def relay_kernel(parts_ref, copies_ref):
    spread(copies_ref, total(parts_ref))


def pair_kernel(own_ref, other_ref, copies_ref):
    spread(copies_ref, own_ref[...] + other_ref[...])


def params_kernel(parts_ref, time_gram_ref, params_ref, gram_ref, space_gram_ref):
    half = params_ref.shape[0] // 2
    whole = total(parts_ref)
    split = whole.shape[0] - 1
    side, space_gram = unfold(whole[:half, :]), unpack(whole[half:split, :], whole[split:, :])
    space_gram_ref[...] = space_gram
    inverse = ridge_inverse(space_gram * time_gram_ref[...])
    params = dot(side, inverse, (1, 0), EXACT)
    params_ref[...] = params
    gram_ref[...] = fold(gram_rows(params))


def time_side_kernel(contracted_ref, params_ref, side_ref):
    samples, rank = params_ref.shape
    steps = 2 * side_ref.shape[0]
    sums = [jnp.zeros((8, rank), F32) for _ in range(steps // 8)]
    for j in range(samples):
        factor = jnp.broadcast_to(params_ref[j : j + 1, :], (8, rank))
        for q in range(steps // 8):
            sums[q] = sums[q] + contracted_ref[j * steps + 8 * q : j * steps + 8 * q + 8, :] * factor
    side_ref[...] = fold(jnp.concatenate(sums, axis=0))


def times_inverse_kernel(own_ref, other_ref, space_gram_ref, inverse_ref, gram_ref):
    gram = unfold(own_ref[...] + other_ref[...])
    gram_ref[...] = gram
    inverse_ref[...] = ridge_inverse(gram * space_gram_ref[...])


def space_inverse_kernel(first_ref, second_ref, inverse_ref):
    inverse_ref[...] = ridge_inverse(first_ref[...] * second_ref[...])


def times_kernel(rows_ref, parts_ref, inverse_ref, params_ref, times_ref, gram_ref, side_ref, khatri_ref):
    steps, rank = times_ref.shape
    samples = params_ref.shape[0]
    times = dot(unfold(total(parts_ref)), inverse_ref[...], (1, 0), EXACT)
    times_ref[...] = times
    gram_ref[...] = gram_rows(times)
    for j in range(samples):
        factor = jnp.broadcast_to(params_ref[j : j + 1, :], times.shape)
        khatri_ref[j * steps : (j + 1) * steps, :] = (times * factor).astype(BF16)
    side_ref[...] = dot(khatri_ref[...], rows_ref[...], (0, 0))


HERE = pl.BlockSpec(memory_space=pltpu.VMEM)
AWAY = pl.BlockSpec(memory_space=pltpu.HBM)


def on_device(kernel, shapes, inputs, scratch=(), limit=8):
    return pl.pallas_call(
        kernel,
        out_shape=[s if isinstance(s, jax.ShapeDtypeStruct) else jax.ShapeDtypeStruct(s, F32) for s in shapes],
        in_specs=[HERE] * inputs if isinstance(inputs, int) else inputs,
        out_specs=[HERE] * len(shapes),
        scratch_shapes=list(scratch),
        compiler_params=pltpu.CompilerParams(vmem_limit_bytes=limit << 20),
    )


def exchange(copies, axes):
    return lax.all_to_all(copies, axes, split_axis=0, concat_axis=0, tiled=True)


def other_core(x):
    return lax.ppermute(x, CORE, [(0, 1), (1, 0)])


def per_device(snapshots, space_start, time_start):
    samples, steps, nodes = snapshots.shape
    rank = space_start.shape[0]
    plane, line = lax.axis_size(PLANE), lax.axis_size(LINE)
    width = 2 * rank
    both = samples // 2 + rank // 4 + 1
    count = samples * steps
    source = snapshots.reshape(count, nodes)
    times = time_start.T
    rows_shape = jax.ShapeDtypeStruct((count, nodes), BF16)
    start = on_device(
        start_kernel,
        [rows_shape, (count, rank), (plane, both, width), (rank, rank)],
        [AWAY, AWAY, AWAY],
        [
            pltpu.VMEM((samples, rank), F32),
            pltpu.VMEM((rank, nodes), F32),
            pltpu.VMEM((steps, rank), F32),
            pltpu.SemaphoreType.DMA((samples // (GROUP * CHUNK),)),
            pltpu.SemaphoreType.DMA((2,)),
        ],
        24,
    )
    again = on_device(
        space_kernel, [(count, rank), (plane, both, width)], 5, [pltpu.VMEM((samples, rank), F32)], 24
    )
    last = on_device(last_kernel, [(rank, nodes)], 3)
    relay_both = on_device(relay_kernel, [(line, both, width)], 1)
    relay_times = on_device(relay_kernel, [(line, steps // 2, width)], 1)
    pair = on_device(pair_kernel, [(plane, steps // 2, width)], 2)
    for_params = on_device(params_kernel, [(samples, rank), (rank // 2, width), (rank, rank)], 2)
    time_side = on_device(time_side_kernel, [(steps // 2, width)], 2)
    times_inverse = on_device(times_inverse_kernel, [(rank, rank), (rank, rank)], 3)
    space_inverse = on_device(space_inverse_kernel, [(rank, rank)], 2)
    for_times = on_device(
        times_kernel, [(steps, rank), (rank, rank), (rank, nodes)], 4, [pltpu.VMEM((count, rank), BF16)], 24
    )
    away = [pltpu.with_memory_space_constraint(x, pltpu.HBM) for x in (source, space_start, times)]
    rows, contracted, message, time_gram = start(*away)
    for sweep in range(SWEEPS):
        (message,) = relay_both(exchange(message, PLANE))
        params, gram, space_gram = for_params(exchange(message, LINE), time_gram)
        other_gram = other_core(gram)
        (side,) = time_side(contracted, params)
        other_side = other_core(side)
        inverse, param_gram = times_inverse(gram, other_gram, space_gram)
        side, other_side, inverse = lax.optimization_barrier((side, other_side, inverse))
        (message,) = pair(side, other_side)
        (message,) = relay_times(exchange(message, PLANE))
        times, time_gram, side = for_times(rows, exchange(message, LINE), inverse, params)
        other = other_core(side)
        (inverse,) = space_inverse(param_gram, time_gram)
        if sweep + 1 < SWEEPS:
            contracted, message = again(rows, side, other, inverse, times)
        else:
            (space,) = last(side, other, inverse)
    return space, params.T, times.T


def solution(mesh):
    split = Mesh(
        mesh.devices.reshape(4, 8, 4, mesh.shape["params"]),
        ("nodes_0", "nodes_1", "nodes_2", "params"),
    )
    return jax.shard_map(
        per_device,
        mesh=split,
        in_specs=(P("params", None, NODES), P(None, NODES), P()),
        out_specs=(P(None, NODES), P(None, "params"), P()),
        check_vma=False,
    )
```

```python
import functools

import jax
import jax.numpy as jnp
from jax import lax
from jax.experimental import pallas as pl
from jax.experimental.pallas import tpu as pltpu
from jax.sharding import Mesh
from jax.sharding import PartitionSpec as P

SWEEPS = 4
NODES = ("nodes_0", "nodes_1", "nodes_2")
PLANE = ("nodes_0", "nodes_2")
LINE = "nodes_1"
CORE = "params"
GROUP = 8
CHUNK = 2
WHOLE = 4
F32 = jnp.float32
BF16 = jnp.bfloat16
EXACT = lax.Precision.HIGHEST
RIDGE_SHARE = 0.01


def dot(a, b, over, precision=None):
    return lax.dot_general(
        a, b, (((over[0],), (over[1],)), ((), ())), precision=precision, preferred_element_type=F32
    )


def gram_rows(a):
    return dot(a, a, (0, 0), EXACT)


def row_of(x, i):
    return jnp.broadcast_to(x[i : i + 1, :], (8, x.shape[1]))


def column_of(x, i):
    return jnp.broadcast_to(x[:, i : i + 1], x.shape)


def eliminate(blocks):
    blocks = list(blocks)
    count = len(blocks)
    sub = lax.broadcasted_iota(jnp.int32, blocks[0].shape, 0)
    for k in range(count):
        lead = [column_of(blocks[k], 8 * k + i) for i in range(8)]
        others = {m: [column_of(blocks[m], 8 * k + i) for i in range(8)] for m in range(count) if m != k}
        rows = blocks[k]
        for i in range(8):
            pivot = sub == i
            factor = jnp.where(pivot, -1.0, lead[i]) * (1.0 / row_of(lead[i], i))
            rows = jnp.where(pivot, 0.0, rows) - factor * row_of(rows, i)
            for n in range(i + 1, 8):
                lead[n] = jnp.where(pivot, 0.0, lead[n]) - factor * row_of(lead[n], i)
        pivots = [row_of(rows, i) for i in range(8)]
        blocks[k] = rows
        for m, columns in others.items():
            terms = [columns[i] * pivots[i] for i in range(8)]
            while len(terms) > 1:
                terms = [terms[i] + terms[i + 1] for i in range(0, len(terms), 2)]
            blocks[m] = blocks[m] - terms[0]
    return blocks


def ridge_inverse(gram):
    n = gram.shape[0]
    row = lax.broadcasted_iota(jnp.int32, (n, n), 0)
    column = lax.broadcasted_iota(jnp.int32, (n, n), 1)
    eye = jnp.where(row == column, 1.0, 0.0).astype(F32)
    trace = jnp.sum(jnp.sum(gram * eye, axis=0, keepdims=True), axis=1, keepdims=True)
    matrix = gram + (RIDGE_SHARE / n) * trace * eye
    both = jnp.concatenate([matrix, eye], axis=1)
    done = eliminate([both[8 * m : 8 * m + 8, :] for m in range(n // 8)])
    return jnp.concatenate(done, axis=0)[:, n:]


def fold(x):
    half = x.shape[0] // 2
    return jnp.concatenate([x[:half, :], x[half:, :]], axis=1)


def unfold(x):
    half = x.shape[1] // 2
    return jnp.concatenate([x[:, :half], x[:, half:]], axis=0)


def pack(gram):
    half = gram.shape[0] // 2
    row = lax.broadcasted_iota(jnp.int32, (half, half), 0)
    column = lax.broadcasted_iota(jnp.int32, (half, half), 1)
    first, cross, last = gram[:half, :half], gram[:half, half:], gram[half:, half:]
    body = fold(jnp.concatenate([jnp.where(row <= column, first, last), cross], axis=1))
    diagonal = jnp.sum(jnp.where(row == column, last, 0.0), axis=0, keepdims=True)
    blank = jnp.zeros((1, body.shape[1] - half), F32)
    return body, jnp.concatenate([diagonal, blank], axis=1)


def unpack(body, tail):
    body = unfold(body)
    half = body.shape[0]
    row = lax.broadcasted_iota(jnp.int32, (half, half), 0)
    column = lax.broadcasted_iota(jnp.int32, (half, half), 1)
    mixed, cross = body[:, :half], body[:, half:]
    turned = mixed.T
    first = jnp.where(row <= column, mixed, turned)
    diagonal = jnp.broadcast_to(tail[:, :half], (half, half))
    last = jnp.where(row > column, mixed, jnp.where(row < column, turned, diagonal))
    return jnp.concatenate(
        [jnp.concatenate([first, cross], axis=1), jnp.concatenate([cross.T, last], axis=1)], axis=0
    )


def total(parts):
    whole = [parts[i] for i in range(parts.shape[0])]
    while len(whole) > 1:
        whole = [whole[i] + whole[i + 1] for i in range(0, len(whole), 2)]
    return whole[0]


def spread(ref, x, rows=slice(None)):
    for i in range(ref.shape[0]):
        ref[i, rows, :] = x


def contract(rows_ref, space, times, contracted_ref, message_ref, side_ref, groups_at_once, arrive=None):
    steps, rank = times.shape
    samples = side_ref.shape[0]
    low = space.astype(BF16)
    body, tail = pack(dot(space, space, (1, 1), EXACT))
    split = samples // 2 + rank // 4
    spread(message_ref, body, slice(samples // 2, split))
    spread(message_ref, tail, slice(split, split + 1))

    def groups(step, carry):
        if arrive is not None:
            arrive(step)
        for group in range(groups_at_once):
            first = pl.multiple_of((step * groups_at_once + group) * GROUP, GROUP)
            here = pl.ds(pl.multiple_of(first * steps, GROUP * steps), GROUP * steps)
            part = dot(rows_ref[here, :], low, (1, 1))
            contracted_ref[here, :] = part
            sides = [
                jnp.sum(part[j * steps : (j + 1) * steps, :] * times, axis=0, keepdims=True) for j in range(GROUP)
            ]
            side_ref[pl.ds(first, GROUP), :] = jnp.concatenate(sides, axis=0)
        return carry

    lax.fori_loop(0, samples // (GROUP * groups_at_once), groups, 0)
    spread(message_ref, fold(side_ref[...]), slice(0, samples // 2))


def start_kernel(
    source_ref,
    space_ref,
    times_ref,
    rows_ref,
    contracted_ref,
    message_ref,
    gram_ref,
    side_ref,
    space_here,
    times_here,
    arrived,
    early,
):
    count = arrived.shape[0]
    size = rows_ref.shape[0] // count
    others = [
        pltpu.make_async_copy(space_ref, space_here, early.at[0]),
        pltpu.make_async_copy(times_ref, times_here, early.at[1]),
    ]
    for copy in others:
        copy.start()

    def load(i):
        here = pl.ds(pl.multiple_of(i * size, size), size)
        return pltpu.make_async_copy(source_ref.at[here, :], rows_ref.at[here, :], arrived.at[i])

    for i in range(count):
        load(i).start()
    for copy in others:
        copy.wait()
    gram_ref[...] = gram_rows(times_here[...])
    contract(
        rows_ref,
        space_here[...],
        times_here[...],
        contracted_ref,
        message_ref,
        side_ref,
        CHUNK,
        lambda step: load(step).wait(),
    )


def space_kernel(rows_ref, own_ref, other_ref, inverse_ref, times_ref, contracted_ref, message_ref, side_ref):
    space = dot(inverse_ref[...], own_ref[...] + other_ref[...], (1, 0), EXACT)
    contract(rows_ref, space, times_ref[...], contracted_ref, message_ref, side_ref, WHOLE)


def last_kernel(own_ref, other_ref, inverse_ref, space_ref):
    space_ref[...] = dot(inverse_ref[...], own_ref[...] + other_ref[...], (1, 0), EXACT)


def relay_kernel(parts_ref, copies_ref):
    spread(copies_ref, total(parts_ref))


def pair_kernel(own_ref, other_ref, copies_ref):
    spread(copies_ref, own_ref[...] + other_ref[...])


def params_kernel(parts_ref, time_gram_ref, params_ref, gram_ref, space_gram_ref):
    half = params_ref.shape[0] // 2
    whole = total(parts_ref)
    split = whole.shape[0] - 1
    side, space_gram = unfold(whole[:half, :]), unpack(whole[half:split, :], whole[split:, :])
    space_gram_ref[...] = space_gram
    inverse = ridge_inverse(space_gram * time_gram_ref[...])
    params = dot(side, inverse, (1, 0), EXACT)
    params_ref[...] = params
    gram_ref[...] = fold(gram_rows(params))


def time_side_kernel(contracted_ref, params_ref, side_ref):
    samples, rank = params_ref.shape
    steps = 2 * side_ref.shape[0]
    sums = [jnp.zeros((8, rank), F32) for _ in range(steps // 8)]
    for j in range(samples):
        factor = jnp.broadcast_to(params_ref[j : j + 1, :], (8, rank))
        for q in range(steps // 8):
            sums[q] = sums[q] + contracted_ref[j * steps + 8 * q : j * steps + 8 * q + 8, :] * factor
    side_ref[...] = fold(jnp.concatenate(sums, axis=0))


def times_inverse_kernel(own_ref, other_ref, space_gram_ref, inverse_ref, gram_ref):
    gram = unfold(own_ref[...] + other_ref[...])
    gram_ref[...] = gram
    inverse_ref[...] = ridge_inverse(gram * space_gram_ref[...])


def space_inverse_kernel(first_ref, second_ref, inverse_ref):
    inverse_ref[...] = ridge_inverse(first_ref[...] * second_ref[...])


def times_kernel(rows_ref, parts_ref, inverse_ref, params_ref, times_ref, gram_ref, side_ref, khatri_ref):
    steps, rank = times_ref.shape
    samples = params_ref.shape[0]
    times = dot(unfold(total(parts_ref)), inverse_ref[...], (1, 0), EXACT)
    times_ref[...] = times
    gram_ref[...] = gram_rows(times)
    for j in range(samples):
        factor = jnp.broadcast_to(params_ref[j : j + 1, :], times.shape)
        khatri_ref[j * steps : (j + 1) * steps, :] = (times * factor).astype(BF16)
    side_ref[...] = dot(khatri_ref[...], rows_ref[...], (0, 0))


HERE = pl.BlockSpec(memory_space=pltpu.VMEM)
AWAY = pl.BlockSpec(memory_space=pltpu.HBM)


def on_device(kernel, shapes, inputs, scratch=(), limit=8):
    return pl.pallas_call(
        kernel,
        out_shape=[s if isinstance(s, jax.ShapeDtypeStruct) else jax.ShapeDtypeStruct(s, F32) for s in shapes],
        in_specs=[HERE] * inputs if isinstance(inputs, int) else inputs,
        out_specs=[HERE] * len(shapes),
        scratch_shapes=list(scratch),
        compiler_params=pltpu.CompilerParams(vmem_limit_bytes=limit << 20),
    )


def exchange(copies, axes):
    return lax.all_to_all(copies, axes, split_axis=0, concat_axis=0, tiled=True)


def other_core(x):
    return lax.ppermute(x, CORE, [(0, 1), (1, 0)])


def per_device(snapshots, space_start, time_start):
    samples, steps, nodes = snapshots.shape
    rank = space_start.shape[0]
    plane, line = lax.axis_size(PLANE), lax.axis_size(LINE)
    width = 2 * rank
    both = samples // 2 + rank // 4 + 1
    count = samples * steps
    source = snapshots.reshape(count, nodes)
    times = time_start.T
    rows_shape = jax.ShapeDtypeStruct((count, nodes), BF16)
    start = on_device(
        start_kernel,
        [rows_shape, (count, rank), (plane, both, width), (rank, rank)],
        [AWAY, AWAY, AWAY],
        [
            pltpu.VMEM((samples, rank), F32),
            pltpu.VMEM((rank, nodes), F32),
            pltpu.VMEM((steps, rank), F32),
            pltpu.SemaphoreType.DMA((samples // (GROUP * CHUNK),)),
            pltpu.SemaphoreType.DMA((2,)),
        ],
        24,
    )
    again = on_device(
        space_kernel, [(count, rank), (plane, both, width)], 5, [pltpu.VMEM((samples, rank), F32)], 24
    )
    last = on_device(last_kernel, [(rank, nodes)], 3)
    relay_both = on_device(relay_kernel, [(line, both, width)], 1)
    relay_times = on_device(relay_kernel, [(line, steps // 2, width)], 1)
    pair = on_device(pair_kernel, [(plane, steps // 2, width)], 2)
    for_params = on_device(params_kernel, [(samples, rank), (rank // 2, width), (rank, rank)], 2)
    time_side = on_device(time_side_kernel, [(steps // 2, width)], 2)
    times_inverse = on_device(times_inverse_kernel, [(rank, rank), (rank, rank)], 3)
    space_inverse = on_device(space_inverse_kernel, [(rank, rank)], 2)
    for_times = on_device(
        times_kernel, [(steps, rank), (rank, rank), (rank, nodes)], 4, [pltpu.VMEM((count, rank), BF16)], 24
    )
    away = [pltpu.with_memory_space_constraint(x, pltpu.HBM) for x in (source, space_start, times)]
    rows, contracted, message, time_gram = start(*away)
    for sweep in range(SWEEPS):
        (message,) = relay_both(exchange(message, PLANE))
        params, gram, space_gram = for_params(exchange(message, LINE), time_gram)
        other_gram = other_core(gram)
        (side,) = time_side(contracted, params)
        other_side = other_core(side)
        inverse, param_gram = times_inverse(gram, other_gram, space_gram)
        side, other_side, inverse = lax.optimization_barrier((side, other_side, inverse))
        (message,) = pair(side, other_side)
        (message,) = relay_times(exchange(message, PLANE))
        times, time_gram, side = for_times(rows, exchange(message, LINE), inverse, params)
        other = other_core(side)
        (inverse,) = space_inverse(param_gram, time_gram)
        if sweep + 1 < SWEEPS:
            contracted, message = again(rows, side, other, inverse, times)
        else:
            (space,) = last(side, other, inverse)
    return space, params.T, times.T


def solution(mesh):
    split = Mesh(
        mesh.devices.reshape(4, 8, 4, mesh.shape["params"]),
        ("nodes_0", "nodes_1", "nodes_2", "params"),
    )
    return jax.shard_map(
        per_device,
        mesh=split,
        in_specs=(P("params", None, NODES), P(None, NODES), P()),
        out_specs=(P(None, NODES), P(None, "params"), P()),
        check_vma=False,
    )
```
